128 devices in a mesh: row: 16 (over z, x), col: 8 (over y, core).
Axes of the slice: x: 4, y: 4, z: 4, core: 2. Of those that a mesh axis runs over, the one named last changes fastest.
Arguments:
- amp_tiles: bfloat16 [2, 8, 64, 256, 256], P(None, 'col', 'row'), may hold values from -6 to 6
- amp_rows: int32 [2, 8, 64], P(None, 'col', 'row'), may hold values from -1 to 3, as said below
- int_tiles: bfloat16 [2, 16, 16, 256, 256], P(None, 'col', 'row'), may hold values from -0.1875 to 0.1875
- int_codes: int32 [2, 16, 16], P(None, 'col', 'row'), may hold values from -1 to 11, as said below
Outputs:
- ladder: float32 [8192, 24576], P('col', 'row')
The draws below stay inside these ranges and needn't reach their ends.
Inputs may be any that keep to these rules, and one draw needn't show every extreme that they name: `amp_rows`: the live tile rows among one device's 4 amplitude slots of a panel are distinct; -1 marks an empty slot. `int_codes`: the live codes among one device's 2 integral slots of a panel are distinct; -1 marks an empty slot.
All inputs are finite; a program needn't handle non-finite values.
Results may differ from the reference program's by a relative error of at most 0.0003.
Values may be sent and summed in bfloat16 or wider, within the bound.
A program may use at most 192 MiB of HBM per device.

```python
import jax
import jax.numpy as jnp
from jax import lax

TL = 256
MI = 4
NJ = 6
SA = 4
SB = 2
STEPS = 2
KB = 2
N_ROW = 16
N_COL = 8


def distinct_pick(key, lead_shape, span_size, pick_count):
    scores = jax.random.randint(key, lead_shape + (span_size,), 0, 1 << 20) * span_size + jnp.arange(span_size, dtype=jnp.int32)
    ranking = jnp.argsort(scores, axis=-1, stable=True).astype(jnp.int32)
    picked = ranking[..., :pick_count]
    vacant = jax.random.randint(jax.random.fold_in(key, 7), lead_shape + (pick_count,), 0, 4) == 0
    return jnp.where(vacant, -1, picked).astype(jnp.int32)


def draw_amp_rows(key, part):
    picked = distinct_pick(jax.random.fold_in(key, 11), (STEPS, N_COL, N_ROW), MI, SA)
    return picked.reshape(STEPS, N_COL, N_ROW * SA)


def draw_int_codes(key, part):
    picked = distinct_pick(jax.random.fold_in(key, 23), (STEPS, N_COL, N_ROW), KB * NJ, SB)
    return jnp.transpose(picked, (0, 1, 3, 2)).reshape(STEPS, N_COL * SB, N_ROW)


def block_scale(rng, extent, shards, low, top_value):
    loudness, own = 1.0, jax.random.fold_in(rng, 6)
    for axis_at, shards_of in shards:
        heights = jnp.exp(jax.random.uniform(jax.random.fold_in(own, axis_at), (shards_of,), jnp.float32, low / len(shards), top_value / len(shards)))
        loudness = loudness * jnp.repeat(heights, extent[axis_at] // shards_of).reshape([-1 if axis == axis_at else 1 for axis in range(len(extent))])
    return loudness


def bell_draw(rng, dims, spread, most, pieces=(), held_as=jnp.bfloat16):
    level = block_scale(rng, dims, pieces, -0.22, 0.18) if pieces else 1.0
    values = jax.random.normal(rng, dims, jnp.float32) * spread * level
    return jnp.minimum(jnp.maximum(values, -most), most).astype(held_as)


def setup_inputs(seed: int = 0) -> dict:
    key_of = jax.random.split(jax.random.key(seed), 5)
    amp_tiles = bell_draw(key_of[0], (STEPS, N_COL, N_ROW * SA, TL, TL), 1.0, 6.0, ((1, 8), (2, 16)))
    amp_rows = draw_amp_rows(jax.random.fold_in(key_of[4], 71), 0)
    int_tiles = bell_draw(key_of[2], (STEPS, N_COL * SB, N_ROW, TL, TL), (TL * 4) ** -0.5, 0.1875, ((1, 8), (2, 16)))
    int_codes = draw_int_codes(jax.random.fold_in(key_of[4], 71), 0)
    return {"amp_tiles": amp_tiles, "amp_rows": amp_rows, "int_tiles": int_tiles, "int_codes": int_codes}


def densify(tiles, codes, per_dev, rows_held, panel_tiles, cols_tiles, width):
    slot_ids = jnp.arange(codes.shape[0], dtype=jnp.int32)
    living = codes >= 0
    k_index = jnp.where(living, (slot_ids // per_dev) * rows_held + codes // cols_tiles, panel_tiles).astype(jnp.int32)
    j_index = jnp.where(living, codes % cols_tiles, 0).astype(jnp.int32)
    dense = jnp.zeros((panel_tiles, width, cols_tiles, width), jnp.bfloat16)
    dense = dense.at[k_index, :, j_index, :].set(tiles, mode="drop")
    return dense.reshape(panel_tiles, width, cols_tiles * width)


def reference(amp_tiles, amp_rows, int_tiles, int_codes):
    total = jnp.zeros((N_COL, MI, TL, N_ROW, NJ * TL), jnp.float32)
    for step in range(STEPS):
        panels = jnp.stack([densify(int_tiles[step, :, rank], int_codes[step, :, rank], SB, KB, N_ROW, NJ, TL) for rank in range(N_ROW)])

        def per_col(items):
            tiles, rows = items

            def one_slot(carry, item):
                tile, tile_rows, slot = item
                k_index = (slot // SA).astype(jnp.int32)
                block = lax.dynamic_index_in_dim(panels, k_index, 1, keepdims=False).astype(jnp.float32)
                product = jnp.einsum("xy,ryz->xrz", tile.astype(jnp.float32), block, precision=lax.Precision.HIGHEST)
                living = (tile_rows >= 0).astype(jnp.float32)
                target = jnp.maximum(tile_rows, 0).astype(jnp.int32)
                current = lax.dynamic_index_in_dim(carry, target, 0, keepdims=False)
                return lax.dynamic_update_index_in_dim(carry, current + living * product, target, 0), None

            start_total = jnp.zeros((MI, TL, N_ROW, NJ * TL), jnp.float32)
            slot_ids = jnp.arange(rows.shape[0], dtype=jnp.int32)
            result, _ = lax.scan(one_slot, start_total, (tiles, rows, slot_ids))
            return result

        total = total + lax.map(per_col, (amp_tiles[step], amp_rows[step]))
    return total.reshape(N_COL * MI * TL, N_ROW * NJ * TL)
```

```python
import jax
import jax.numpy as jnp
from jax import lax
from jax.experimental import pallas as pl
from jax.experimental.pallas import tpu as pltpu
from jax.sharding import PartitionSpec as P

TL = 256
MI = 4
NJ = 6
SA = 4
SB = 2
STEPS = 2
KB = 2
RING = 4
PLUS, MINUS = 0, 1
LANDS = (RING - 1, 1)
HALF = SA // 2


def place():
    row, col = lax.axis_index("row"), lax.axis_index("col")
    return row // RING, row % RING, col // 2, col % 2


def gather_kernel(a_ref, b_ref, rows_ref, codes_ref, a_out, b_out, rows_out, codes_out,
                  a_send, a_recv, b_send, b_recv, m_send, m_recv, own_sem):
    z, x, y, core = place()
    row, col = lax.axis_index("row"), lax.axis_index("col")
    near = lambda v, d: lax.rem(v + (1 if d == PLUS else RING - 1), RING)
    x_dev = [(z * RING + near(x, d), col) for d in (PLUS, MINUS)]
    z_dev = [(near(z, d) * RING + x, col) for d in (PLUS, MINUS)]
    y_dev = [(row, near(y, d) * 2 + core) for d in (PLUS, MINUS)]
    mate = (row, y * 2 + 1 - core)
    first = (x_dev, z_dev)
    second = (z_dev, x_dev)

    barrier = pltpu.get_barrier_semaphore()
    for dev in x_dev + z_dev + y_dev + [mate]:
        pl.semaphore_signal(barrier, inc=1, device_id=dev, device_id_type=pl.DeviceIdType.MESH)
    pl.semaphore_wait(barrier, 7)

    sends = []

    def send(src, dst, ssem, rsem, dev):
        copy = pltpu.make_async_remote_copy(
            src_ref=src, dst_ref=dst, send_sem=ssem, recv_sem=rsem,
            device_id=dev, device_id_type=pl.DeviceIdType.MESH)
        copy.start()
        sends.append(copy)

    def arrived(dst, rsem):
        pltpu.make_async_copy(dst, dst, rsem).wait()

    def a_at(p, ds, df, h):
        return a_out.at[p, ds, df, pl.ds(h * HALF, HALF)]

    def a_first(p, d, h):
        send(a_ref.at[p, pl.ds(h * HALF, HALF)], a_at(p, 0, LANDS[d], h),
             a_send.at[p, d, h], a_recv.at[p, d, h], first[p][d])

    def a_first_got(p, d, h):
        arrived(a_at(p, 0, LANDS[d], h), a_recv.at[p, d, h])

    def a_first_relay(p, d):
        send(a_at(p, 0, LANDS[d], d), a_at(p, 0, 2, d),
             a_send.at[p, d, 2], a_recv.at[p, d, 2], first[p][d])

    def a_first_relay_got(p, d):
        arrived(a_at(p, 0, 2, d), a_recv.at[p, d, 2])

    def a_second(p, d, df, h):
        src = a_ref.at[p, pl.ds(h * HALF, HALF)] if df == 0 else a_at(p, 0, df, h)
        send(src, a_at(p, LANDS[d], df, h),
             a_send.at[p, d, 3 + df * 3 + h], a_recv.at[p, d, 3 + df * 3 + h], second[p][d])

    def a_second_got(p, d, df, h):
        arrived(a_at(p, LANDS[d], df, h), a_recv.at[p, d, 3 + df * 3 + h])

    def a_second_relay(p, d, df):
        send(a_at(p, LANDS[d], df, d), a_at(p, 2, df, d),
             a_send.at[p, d, 5 + df * 3], a_recv.at[p, d, 5 + df * 3], second[p][d])

    def a_second_relay_got(p, d, df):
        arrived(a_at(p, 2, df, d), a_recv.at[p, d, 5 + df * 3])

    both = [(p, d) for p in range(STEPS) for d in (PLUS, MINUS)]

    for d in (PLUS, MINUS):
        send(rows_ref, rows_out.at[0, LANDS[d]], m_send.at[d], m_recv.at[d], x_dev[d])
        send(codes_ref, codes_out.at[0, LANDS[d]], m_send.at[6 + d], m_recv.at[6 + d], y_dev[d])
    send(codes_ref, codes_out.at[1, 0], m_send.at[9], m_recv.at[9], mate)
    for p, d in both:
        a_first(p, d, d)
    for d in (PLUS, MINUS):
        send(b_ref.at[d], b_out.at[0, LANDS[d], d], b_send.at[d, d], b_recv.at[d, d], y_dev[d])
    for p, d in both:
        a_first(p, d, 1 - d)
    for d in (PLUS, MINUS):
        send(b_ref.at[1 - d], b_out.at[0, LANDS[d], 1 - d], b_send.at[d, 1 - d], b_recv.at[d, 1 - d], y_dev[d])
    send(b_ref, b_out.at[1, 0], b_send.at[2, 0], b_recv.at[2, 0], mate)
    for p, d in both:
        a_second(p, d, 0, d)
    for p, d in both:
        a_second(p, d, 0, 1 - d)

    own = [pltpu.make_async_copy(a_ref.at[p], a_out.at[p, 0, 0], own_sem.at[p]) for p in range(STEPS)]
    own.append(pltpu.make_async_copy(b_ref, b_out.at[0, 0], own_sem.at[2]))
    own.append(pltpu.make_async_copy(rows_ref, rows_out.at[0, 0], own_sem.at[3]))
    own.append(pltpu.make_async_copy(codes_ref, codes_out.at[0, 0], own_sem.at[4]))
    for copy in own:
        copy.start()

    for d in (PLUS, MINUS):
        arrived(rows_out.at[0, LANDS[d]], m_recv.at[d])
        arrived(codes_out.at[0, LANDS[d]], m_recv.at[6 + d])
    send(rows_out.at[0, LANDS[PLUS]], rows_out.at[0, 2], m_send.at[2], m_recv.at[2], x_dev[PLUS])
    send(codes_out.at[0, LANDS[PLUS]], codes_out.at[0, 2], m_send.at[8], m_recv.at[8], y_dev[PLUS])

    for p, d in both:
        a_first_got(p, d, d)
        a_first_relay(p, d)
    for d in (PLUS, MINUS):
        arrived(b_out.at[0, LANDS[d], d], b_recv.at[d, d])
        send(b_out.at[0, LANDS[d], d], b_out.at[0, 2, d], b_send.at[d, 2], b_recv.at[d, 2], y_dev[d])
    for copy in own:
        copy.wait()
    arrived(rows_out.at[0, 2], m_recv.at[2])
    arrived(codes_out.at[0, 2], m_recv.at[8])
    for d in (PLUS, MINUS):
        send(rows_out.at[0], rows_out.at[LANDS[d]], m_send.at[3 + d], m_recv.at[3 + d], z_dev[d])
    send(codes_out.at[0, pl.ds(1, 3)], codes_out.at[1, pl.ds(1, 3)], m_send.at[10], m_recv.at[10], mate)

    for p, d in both:
        a_first_got(p, d, 1 - d)
    for df in (LANDS[PLUS], LANDS[MINUS]):
        for p, d in both:
            a_second(p, d, df, d)
        for p, d in both:
            a_second(p, d, df, 1 - d)
    for d in (PLUS, MINUS):
        arrived(b_out.at[0, LANDS[d], 1 - d], b_recv.at[d, 1 - d])
        send(b_out.at[0, LANDS[d]], b_out.at[1, LANDS[d]], b_send.at[2, LANDS[d]], b_recv.at[2, LANDS[d]], mate)
    for p, d in both:
        a_second_got(p, d, 0, d)
        a_second_relay(p, d, 0)
    for p, d in both:
        a_first_relay_got(p, d)
    for p, d in both:
        a_second(p, d, 2, d)
    for p, d in both:
        a_second(p, d, 2, 1 - d)
    for d in (PLUS, MINUS):
        arrived(b_out.at[0, 2, d], b_recv.at[d, 2])
    send(b_out.at[0, 2], b_out.at[1, 2], b_send.at[2, 2], b_recv.at[2, 2], mate)
    for d in (PLUS, MINUS):
        arrived(rows_out.at[LANDS[d]], m_recv.at[3 + d])
    send(rows_out.at[LANDS[PLUS]], rows_out.at[2], m_send.at[5], m_recv.at[5], z_dev[PLUS])
    for df in (LANDS[PLUS], LANDS[MINUS], 2):
        for p, d in both:
            a_second_got(p, d, df, d)
            a_second_relay(p, d, df)

    arrived(codes_out.at[1, 0], m_recv.at[9])
    arrived(codes_out.at[1, pl.ds(1, 3)], m_recv.at[10])
    arrived(rows_out.at[2], m_recv.at[5])
    for dy in range(RING):
        arrived(b_out.at[1, dy], b_recv.at[2, dy])
    for df in range(RING):
        for p, d in both:
            a_second_got(p, d, df, 1 - d)
            a_second_relay_got(p, d, df)
    for copy in sends:
        copy.wait_send()


def multiply_kernel(rows_ref, codes_ref, a_ref, b_ref, o_ref, acc):
    z, x, y, core = place()
    acc[...] = jnp.zeros_like(acc)

    @pl.loop(0, STEPS * 2 * RING * SB)
    def _(n):
        t = n % SB
        dy = (n // SB) % RING
        dc = (n // (SB * RING)) % 2
        p = n // (SB * RING * 2)
        code = codes_ref[dc, dy, p, t]

        @pl.when(code >= 0)
        def _():
            owner = ((y + dy) % RING) * 2 + (core + dc) % 2
            k = owner * KB + code // NJ
            j = code % NJ
            dz = (k // RING - z + RING) % RING
            dx = (k % RING - x + RING) % RING
            ds = jnp.where(p == 0, dz, dx)
            df = jnp.where(p == 0, dx, dz)
            tile = b_ref[dc, dy, p, t]
            for u in range(SA):
                target = rows_ref[dz, dx, p, u]

                @pl.when(target >= 0)
                def _():
                    at = (pl.ds(pl.multiple_of(target * TL, TL), TL), pl.ds(pl.multiple_of(j * TL, TL), TL))
                    acc[at] += jnp.dot(a_ref[p, ds, df, u], tile, preferred_element_type=jnp.float32)

    pltpu.sync_copy(acc, o_ref)


def body(amp_tiles, amp_rows, int_tiles, int_codes):
    a = amp_tiles.reshape(STEPS, SA, TL, TL)
    b = int_tiles.reshape(STEPS, SB, TL, TL)
    rows = amp_rows.reshape(STEPS, SA)
    codes = int_codes.reshape(STEPS, SB)
    hbm = pl.BlockSpec(memory_space=pl.ANY)
    a_all, b_all, rows_all, codes_all = pl.pallas_call(
        gather_kernel,
        out_shape=(
            jax.ShapeDtypeStruct((STEPS, RING, RING, SA, TL, TL), jnp.bfloat16),
            jax.ShapeDtypeStruct((2, RING, STEPS, SB, TL, TL), jnp.bfloat16),
            jax.ShapeDtypeStruct((RING, RING, STEPS, SA), jnp.int32),
            jax.ShapeDtypeStruct((2, RING, STEPS, SB), jnp.int32),
        ),
        in_specs=[hbm] * 4,
        out_specs=(hbm,) * 4,
        scratch_shapes=[
            pltpu.SemaphoreType.DMA((STEPS, 2, 15)),
            pltpu.SemaphoreType.DMA((STEPS, 2, 15)),
            pltpu.SemaphoreType.DMA((3, RING)),
            pltpu.SemaphoreType.DMA((3, RING)),
            pltpu.SemaphoreType.DMA((11,)),
            pltpu.SemaphoreType.DMA((11,)),
            pltpu.SemaphoreType.DMA((5,)),
        ],
        compiler_params=pltpu.CompilerParams(collective_id=0, has_side_effects=True),
        name="gather",
    )(a, b, rows, codes)
    smem = pl.BlockSpec(memory_space=pltpu.SMEM)
    vmem = pl.BlockSpec(memory_space=pltpu.VMEM)
    return pl.pallas_call(
        multiply_kernel,
        out_shape=jax.ShapeDtypeStruct((MI * TL, NJ * TL), jnp.float32),
        in_specs=[smem, smem, vmem, vmem],
        out_specs=hbm,
        scratch_shapes=[pltpu.VMEM((MI * TL, NJ * TL), jnp.float32)],
        compiler_params=pltpu.CompilerParams(vmem_limit_bytes=50 * 2**20),
        name="multiply",
    )(rows_all, codes_all, a_all, b_all)


def solution(mesh):
    return jax.shard_map(
        body,
        mesh=mesh,
        in_specs=(
            P(None, "col", "row", None, None),
            P(None, "col", "row"),
            P(None, "col", "row", None, None),
            P(None, "col", "row"),
        ),
        out_specs=P("col", "row"),
        check_vma=False,
    )
```

```python
import jax
import jax.numpy as jnp
from jax import lax
from jax.experimental import pallas as pl
from jax.experimental.pallas import tpu as pltpu
from jax.sharding import PartitionSpec as P

TL = 256
MI = 4
NJ = 6
SA = 4
SB = 2
STEPS = 2
KB = 2
RING = 4
PLUS, MINUS = 0, 1
LANDS = (RING - 1, 1)
HALF = SA // 2
MESH = pl.DeviceIdType.MESH


def gather_kernel(a_ref, b_ref, rows_ref, codes_ref, acc, a_cat, b_cat,
                  a_all, b_all, rows_all, codes_all, rows_s, codes_s,
                  a_send, a_recv, b_send, b_recv, m_send, m_recv, own_sem):
    row, col = lax.axis_index("row"), lax.axis_index("col")
    z, x, y, core = row // RING, row % RING, col // 2, col % 2
    near = lambda v, d: lax.rem(v + (1 if d == PLUS else RING - 1), RING)
    x_dev = [(z * RING + near(x, d), col) for d in (PLUS, MINUS)]
    z_dev = [(near(z, d) * RING + x, col) for d in (PLUS, MINUS)]
    y_dev = [(row, near(y, d) * 2 + core) for d in (PLUS, MINUS)]
    mate = (row, y * 2 + 1 - core)
    first = (x_dev, z_dev)
    second = (z_dev, x_dev)
    dirs = (PLUS, MINUS)
    both = [(p, d) for p in range(STEPS) for d in dirs]

    own = [
        pltpu.make_async_copy(a_ref, a_all.at[:, 0, 0], own_sem.at[0]),
        pltpu.make_async_copy(b_ref, b_all.at[0, 0], own_sem.at[1]),
        pltpu.make_async_copy(rows_ref, rows_all.at[0, 0], own_sem.at[2]),
        pltpu.make_async_copy(codes_ref, codes_all.at[0, 0], own_sem.at[3]),
    ]
    for copy in own:
        copy.start()
    barrier = pltpu.get_barrier_semaphore()
    for dev in x_dev + z_dev + y_dev + [mate]:
        pl.semaphore_signal(barrier, inc=1, device_id=dev, device_id_type=MESH)
    pl.semaphore_wait(barrier, 7)

    sends = []

    def send(src, dst, ssem, rsem, dev):
        copy = pltpu.make_async_remote_copy(
            src_ref=src, dst_ref=dst, send_sem=ssem, recv_sem=rsem, device_id=dev, device_id_type=MESH)
        copy.start()
        sends.append(copy)

    def arrived(dst, rsem):
        pltpu.make_async_copy(dst, dst, rsem).wait()

    def a_at(p, ds, df, h):
        return a_all.at[p, ds, df, pl.ds(h * HALF, HALF)]

    def own_half(p, h):
        return a_ref.at[p, pl.ds(h * HALF, HALF)]

    def first_send(p, d, h):
        send(own_half(p, h), a_at(p, 0, LANDS[d], h), a_send.at[p, d, h], a_recv.at[p, d, h], first[p][d])

    def first_got(p, d, h):
        arrived(a_at(p, 0, LANDS[d], h), a_recv.at[p, d, h])

    def first_relay(p, d):
        send(a_at(p, 0, LANDS[d], d), a_at(p, 0, 2, d), a_send.at[p, d, 2], a_recv.at[p, d, 2], first[p][d])

    def first_relay_got(p, d):
        arrived(a_at(p, 0, 2, d), a_recv.at[p, d, 2])

    def second_send(p, d, df, h):
        n = 3 + df * 3 + h
        src = own_half(p, h) if df == 0 else a_at(p, 0, df, h)
        send(src, a_at(p, LANDS[d], df, h), a_send.at[p, d, n], a_recv.at[p, d, n], second[p][d])

    def second_got(p, d, df, h):
        arrived(a_at(p, LANDS[d], df, h), a_recv.at[p, d, 3 + df * 3 + h])

    def second_relay(p, d, df):
        n = 5 + df * 3
        send(a_at(p, LANDS[d], df, d), a_at(p, 2, df, d), a_send.at[p, d, n], a_recv.at[p, d, n], second[p][d])

    def second_relay_got(p, d, df):
        arrived(a_at(p, 2, df, d), a_recv.at[p, d, 5 + df * 3])

    def second_block(df):
        for p, d in both:
            second_send(p, d, df, d)
        for p, d in both:
            second_send(p, d, df, 1 - d)

    def lay_out(ds, df):
        for p in range(STEPS):
            zo = lax.rem(z + (ds, df)[p], RING)
            xo = lax.rem(x + (df, ds)[p], RING)
            dy = lax.rem(zo + RING - y, RING)
            dc = lax.rem(xo // 2 + core, 2)
            base = lax.rem(xo, 2) * NJ
            dz, dx = (ds, df)[p], (df, ds)[p]
            zero = jnp.zeros((TL, TL), jnp.bfloat16)

            @pl.loop(0, MI)
            def _(i):
                tile = zero
                for u in range(SA):
                    tile = jnp.where(rows_s[dz, dx, p, u] == i, a_all[p, ds, df, u], tile)
                a_cat[pl.ds(pl.multiple_of(i * TL, TL), TL), p * TL:(p + 1) * TL] = tile

            @pl.loop(0, NJ)
            def _(j):
                tile = zero
                for t in range(SB):
                    tile = jnp.where(codes_s[dc, dy, p, t] == base + j, b_all[dc, dy, p, t], tile)
                b_cat[p * TL:(p + 1) * TL, pl.ds(pl.multiple_of(j * TL, TL), TL)] = tile

    def multiply(ds, df, begin=False):
        lay_out(ds, df)

        @pl.loop(0, MI)
        def _(i):
            at = pl.ds(pl.multiple_of(i * TL, TL), TL)
            product = jnp.dot(a_cat[at, :], b_cat[...], preferred_element_type=jnp.float32)
            if begin:
                acc[at, :] = product
            else:
                acc[at, :] += product

    for d in dirs:
        send(rows_ref, rows_all.at[0, LANDS[d]], m_send.at[d], m_recv.at[d], x_dev[d])
        send(codes_ref, codes_all.at[0, LANDS[d]], m_send.at[6 + d], m_recv.at[6 + d], y_dev[d])
    send(codes_ref, codes_all.at[1, 0], m_send.at[9], m_recv.at[9], mate)
    for p, d in both:
        first_send(p, d, d)
    for d in dirs:
        send(b_ref.at[d], b_all.at[0, LANDS[d], d], b_send.at[d, d], b_recv.at[d, d], y_dev[d])
    send(b_ref, b_all.at[1, 0], b_send.at[2, 0], b_recv.at[2, 0], mate)

    for copy in own:
        copy.wait()
    for d in dirs:
        arrived(rows_all.at[0, LANDS[d]], m_recv.at[d])
        arrived(codes_all.at[0, LANDS[d]], m_recv.at[6 + d])
    send(rows_all.at[0, LANDS[PLUS]], rows_all.at[0, 2], m_send.at[2], m_recv.at[2], x_dev[PLUS])
    send(codes_all.at[0, LANDS[PLUS]], codes_all.at[0, 2], m_send.at[8], m_recv.at[8], y_dev[PLUS])
    for p, d in both:
        first_send(p, d, 1 - d)
    for d in dirs:
        send(b_ref.at[1 - d], b_all.at[0, LANDS[d], 1 - d], b_send.at[d, 1 - d], b_recv.at[d, 1 - d], y_dev[d])

    arrived(rows_all.at[0, 2], m_recv.at[2])
    for d in dirs:
        send(rows_all.at[0], rows_all.at[LANDS[d]], m_send.at[3 + d], m_recv.at[3 + d], z_dev[d])
    for p, d in both:
        first_got(p, d, d)
        first_relay(p, d)
    arrived(codes_all.at[0, 2], m_recv.at[8])
    send(codes_all.at[0, pl.ds(1, 3)], codes_all.at[1, pl.ds(1, 3)], m_send.at[10], m_recv.at[10], mate)
    for d in dirs:
        arrived(b_all.at[0, LANDS[d], d], b_recv.at[d, d])
        send(b_all.at[0, LANDS[d], d], b_all.at[0, 2, d], b_send.at[d, 2], b_recv.at[d, 2], y_dev[d])

    for d in dirs:
        arrived(rows_all.at[LANDS[d]], m_recv.at[3 + d])
    send(rows_all.at[LANDS[PLUS]], rows_all.at[2], m_send.at[5], m_recv.at[5], z_dev[PLUS])
    second_block(0)
    for p, d in both:
        first_got(p, d, 1 - d)
    second_block(LANDS[PLUS])
    second_block(LANDS[MINUS])
    for d in dirs:
        arrived(b_all.at[0, LANDS[d], 1 - d], b_recv.at[d, 1 - d])
        send(b_all.at[0, LANDS[d]], b_all.at[1, LANDS[d]], b_send.at[2, LANDS[d]], b_recv.at[2, LANDS[d]], mate)
    for d in dirs:
        arrived(b_all.at[0, 2, d], b_recv.at[d, 2])
    send(b_all.at[0, 2], b_all.at[1, 2], b_send.at[2, 2], b_recv.at[2, 2], mate)

    arrived(codes_all.at[1, 0], m_recv.at[9])
    arrived(codes_all.at[1, pl.ds(1, 3)], m_recv.at[10])
    arrived(rows_all.at[2], m_recv.at[5])
    tables = [pltpu.make_async_copy(rows_all, rows_s, own_sem.at[4]),
              pltpu.make_async_copy(codes_all, codes_s, own_sem.at[5])]
    for copy in tables:
        copy.start()
    for copy in tables:
        copy.wait()
    for dy in range(RING):
        arrived(b_all.at[1, dy], b_recv.at[2, dy])

    multiply(0, 0, begin=True)
    multiply(0, LANDS[PLUS])
    multiply(0, LANDS[MINUS])
    for p, d in both:
        second_got(p, d, 0, d)
        second_relay(p, d, 0)
    for p, d in both:
        first_relay_got(p, d)
    second_block(2)
    multiply(0, 2)
    for p, d in both:
        second_got(p, d, 0, 1 - d)
    multiply(LANDS[PLUS], 0)
    multiply(LANDS[MINUS], 0)
    for df in LANDS:
        for p, d in both:
            second_got(p, d, df, d)
            second_relay(p, d, df)
        for p, d in both:
            second_got(p, d, df, 1 - d)
        multiply(LANDS[PLUS], df)
        multiply(LANDS[MINUS], df)
    for p, d in both:
        second_relay_got(p, d, 0)
    multiply(2, 0)
    for p, d in both:
        second_got(p, d, 2, d)
        second_relay(p, d, 2)
    for p, d in both:
        second_got(p, d, 2, 1 - d)
    multiply(LANDS[PLUS], 2)
    multiply(LANDS[MINUS], 2)
    for df in LANDS:
        for p, d in both:
            second_relay_got(p, d, df)
        multiply(2, df)
    for p, d in both:
        second_relay_got(p, d, 2)
    lay_out(2, 2)
    for copy in sends:
        copy.wait_send()


def finish_kernel(acc, a_cat, b_cat, o_ref, stage, sems):
    copies = []
    for i in range(MI):
        at = pl.ds(i * TL, TL)
        stage[i] = acc[at, :] + jnp.dot(a_cat[at, :], b_cat[...], preferred_element_type=jnp.float32)
        copy = pltpu.make_async_copy(stage.at[i], o_ref.at[at], sems.at[i])
        copy.start()
        copies.append(copy)
    for copy in copies:
        copy.wait()


def body(amp_tiles, amp_rows, int_tiles, int_codes):
    hbm = pl.BlockSpec(memory_space=pltpu.HBM)
    vmem = pl.BlockSpec(memory_space=pltpu.VMEM)
    rows, cols, depth = MI * TL, NJ * TL, STEPS * TL
    totals = pl.pallas_call(
        gather_kernel,
        out_shape=(
            pltpu.VMEM((rows, cols), jnp.float32),
            pltpu.VMEM((rows, depth), jnp.bfloat16),
            pltpu.VMEM((depth, cols), jnp.bfloat16),
        ),
        in_specs=[hbm] * 4,
        out_specs=(vmem,) * 3,
        scratch_shapes=[
            pltpu.VMEM((STEPS, RING, RING, SA, TL, TL), jnp.bfloat16),
            pltpu.VMEM((2, RING, STEPS, SB, TL, TL), jnp.bfloat16),
            pltpu.VMEM((RING, RING, STEPS, SA), jnp.int32),
            pltpu.VMEM((2, RING, STEPS, SB), jnp.int32),
            pltpu.SMEM((RING, RING, STEPS, SA), jnp.int32),
            pltpu.SMEM((2, RING, STEPS, SB), jnp.int32),
            pltpu.SemaphoreType.DMA((STEPS, 2, 15)),
            pltpu.SemaphoreType.DMA((STEPS, 2, 15)),
            pltpu.SemaphoreType.DMA((3, RING)),
            pltpu.SemaphoreType.DMA((3, RING)),
            pltpu.SemaphoreType.DMA((11,)),
            pltpu.SemaphoreType.DMA((11,)),
            pltpu.SemaphoreType.DMA((6,)),
        ],
        compiler_params=pltpu.CompilerParams(
            collective_id=0, has_side_effects=True, vmem_limit_bytes=55 * 2**20),
        name="gather",
    )(
        amp_tiles.reshape(STEPS, SA, TL, TL),
        int_tiles.reshape(STEPS, SB, TL, TL),
        amp_rows.reshape(STEPS, SA),
        int_codes.reshape(STEPS, SB),
    )
    return pl.pallas_call(
        finish_kernel,
        out_shape=jax.ShapeDtypeStruct((rows, cols), jnp.float32),
        in_specs=[vmem] * 3,
        out_specs=hbm,
        scratch_shapes=[pltpu.VMEM((MI, TL, cols), jnp.float32), pltpu.SemaphoreType.DMA((MI,))],
        compiler_params=pltpu.CompilerParams(vmem_limit_bytes=16 * 2**20),
        name="finish",
    )(*totals)


def solution(mesh):
    return jax.shard_map(
        body,
        mesh=mesh,
        in_specs=(
            P(None, "col", "row", None, None),
            P(None, "col", "row"),
            P(None, "col", "row", None, None),
            P(None, "col", "row"),
        ),
        out_specs=P("col", "row"),
        check_vma=False,
    )
```
